128 devices in a mesh: enc: 4 (over y_lo, core), seq: 32 (over x, y_hi, z).
Axes of the slice: x: 4, y: 4 (y_hi: 2, y_lo: 2; y = y_hi * 2 + y_lo), z: 4, core: 2. Of those that a mesh axis runs over, the one named last changes fastest.
Arguments:
- hidden: bfloat16 [8192, 4096], P('seq'), may hold values from -6 to 6
- dec_gain: float32 [4096], replicated, may hold values from 0.1 to 1.9
- cca_query: bfloat16 [4096, 4096], P(None, 'enc'), may hold values from -0.5 to 0.5
- cca_key: bfloat16 [896, 4096], P(None, 'enc'), may hold values from -0.5 to 0.5
- cca_value: bfloat16 [896, 4096], P(None, 'enc'), may hold values from -0.1875 to 0.1875
- cca_out: bfloat16 [4096, 4096], P('enc'), may hold values from -0.09375 to 0.09375
- neighbours: bfloat16 [32, 8, 128, 896], P('seq', 'enc'), may hold values from -6 to 6
- enc_gain: float32 [896], replicated, may hold values from 0.1 to 1.9
- enc_query: bfloat16 [896, 896], P('enc'), may hold values from -0.5 to 0.5
- enc_key: bfloat16 [896, 896], P('enc'), may hold values from -0.5 to 0.5
- enc_value: bfloat16 [896, 896], P('enc'), may hold values from -0.1875 to 0.1875
- enc_output: bfloat16 [896, 896], P('enc'), may hold values from -0.1875 to 0.1875
- enc_cotangent: bfloat16 [32, 8, 128, 896], P('seq', 'enc'), may hold values from -6 to 6
- neighbour_ids: int32 [128, 2], P('seq'), may hold values from 0 to 7, as said below
Outputs:
- mixed: bfloat16 [8192, 4096], P('seq', 'enc')
- d_neighbours: bfloat16 [32, 8, 128, 896], P('seq', 'enc')
- grad_query: float32 [896, 896], P(('enc', 'seq'))
- grad_key: float32 [896, 896], P(('enc', 'seq'))
- grad_value: float32 [896, 896], P(('enc', 'seq'))
- grad_out: float32 [896, 896], P(('enc', 'seq'))
The draws below stay inside these ranges and needn't reach their ends.
Inputs may be any that keep to these rules, and one draw needn't show every extreme that they name: `neighbour_ids`: within each aligned block of 4 stretches every position 0 to 7 appears exactly once.
All inputs are finite; a program needn't handle non-finite values.
Results may differ from the reference program's by a relative error of at most 0.025.
Values may be sent and summed in bfloat16 or wider, within the bound.
No kernel may reach another device: no remote copies, remote signals or barrier semaphores. Data moves between devices by JAX's collectives and lax.ppermute only.
A program may use at most 192 MiB of HBM per device.

```python
import math
import jax
import jax.numpy as jnp
from jax import lax

D = 4096
HD = 128
DE = 896
EHEADS = 14
EHD = 64
C = 64
R = 128
K = 2
SEQ_LEN = 2048
CH_DEV = 4
TOK_DEV = 256
COLUMNS = 32
STRETCHES = 128
TOKENS = 8192


def pair_draw(key):
    key_base, key_other = jax.random.split(jax.random.fold_in(key, 31), 2)
    base_draw = jnp.clip(jax.random.normal(key_base, (DE, DE), jnp.float32), -6.0, 6.0) / math.sqrt(DE)
    other_draw = jnp.clip(jax.random.normal(key_other, (DE, DE), jnp.float32), -6.0, 6.0) / math.sqrt(DE)
    first_out = base_draw
    second_out = other_draw
    return (jnp.clip(first_out, -0.5, 0.5), jnp.clip(second_out, -0.5, 0.5))


def draw_enc_query(key, part):
    return pair_draw(key)[0].astype(jnp.bfloat16)


def draw_enc_key(key, part):
    return pair_draw(key)[1].astype(jnp.bfloat16)


def draw_cca_query(key, part):
    base_draw = jnp.clip(jax.random.normal(jax.random.fold_in(key, 53), (D, D), jnp.float32), -6.0, 6.0) / math.sqrt(D)
    return jnp.clip(base_draw, -0.5, 0.5).astype(jnp.bfloat16)


def draw_cca_key(key, part):
    base_draw = jnp.clip(jax.random.normal(jax.random.fold_in(key, 59), (DE, D), jnp.float32), -6.0, 6.0) / math.sqrt(DE)
    return jnp.clip(base_draw, -0.5, 0.5).astype(jnp.bfloat16)


def draw_neighbour_ids(key, part):
    block_keys = jax.random.split(jax.random.fold_in(key, 5), STRETCHES // CH_DEV)
    blocks = jax.vmap(lambda block_key: jax.random.permutation(block_key, CH_DEV * K))(block_keys)
    return blocks.reshape(STRETCHES, K).astype(jnp.int32)


def block_levels(own_key, extent, cuts, smallest, high):
    def one(dim, shards_of):
        draws = jax.random.uniform(jax.random.fold_in(jax.random.fold_in(own_key, 6), dim), (shards_of,), jnp.float32, smallest / len(cuts), high / len(cuts))
        return jnp.repeat(jnp.exp(draws), extent[dim] // shards_of).reshape((-1,) + (1,) * (len(extent) - dim - 1))

    gain = one(*cuts[0])
    for cut in cuts[1:]:
        gain = gain * one(*cut)
    return gain


def bell_draw(key, dims, scale, most, shards=(), kind=jnp.bfloat16):
    array = jax.random.normal(key, dims, jnp.float32) * scale
    if len(shards) > 0:
        array = block_levels(key, dims, shards, -0.22, 0.18) * array
    return jnp.clip(array, min=-most, max=most).astype(kind)


def setup_inputs(seed: int = 0) -> dict:
    streams_of = jax.random.split(jax.random.key(seed), 15)
    hidden = bell_draw(streams_of[0], (TOKENS, D), 1.0, 6.0, ((0, 32),))
    dec_gain = jnp.clip(1.0 + 0.18 * jax.random.normal(streams_of[1], (D,), jnp.float32), 0.1, 1.9)
    cca_query = draw_cca_query(jax.random.fold_in(streams_of[14], 71), 0)
    cca_key = draw_cca_key(jax.random.fold_in(streams_of[14], 71), 0)
    cca_value = bell_draw(streams_of[4], (DE, D), DE ** -0.5, 0.1875, ((1, 4),))
    cca_out = bell_draw(streams_of[5], (D, D), D ** -0.5, 0.09375, ((0, 4),))
    neighbours = bell_draw(streams_of[6], (COLUMNS, CH_DEV * K, R, DE), 1.0, 6.0, ((0, 32), (1, 4)))
    enc_gain = jnp.clip(1.0 + 0.18 * jax.random.normal(streams_of[7], (DE,), jnp.float32), 0.1, 1.9)
    enc_query = draw_enc_query(jax.random.fold_in(streams_of[14], 71), 0)
    enc_key = draw_enc_key(jax.random.fold_in(streams_of[14], 71), 0)
    enc_value = bell_draw(streams_of[10], (DE, DE), DE ** -0.5, 0.1875, ((0, 4),))
    enc_output = bell_draw(streams_of[11], (DE, DE), DE ** -0.5, 0.1875, ((0, 4),))
    enc_cotangent = bell_draw(streams_of[12], (COLUMNS, CH_DEV * K, R, DE), 1.0, 6.0, ((0, 32), (1, 4)))
    neighbour_ids = draw_neighbour_ids(jax.random.fold_in(streams_of[14], 71), 0)
    return {"hidden": hidden, "dec_gain": dec_gain, "cca_query": cca_query, "cca_key": cca_key, "cca_value": cca_value, "cca_out": cca_out, "neighbours": neighbours, "enc_gain": enc_gain, "enc_query": enc_query, "enc_key": enc_key, "enc_value": enc_value, "enc_output": enc_output, "enc_cotangent": enc_cotangent, "neighbour_ids": neighbour_ids}


EPS = 1e-06

def batched(pattern, former, latter):
    return jnp.einsum(pattern, former.astype(jnp.float32), latter.astype(jnp.float32))

def matmul(former, latter):
    return jnp.dot(former, latter, preferred_element_type=jnp.float32)

def inner_rows(former, latter):
    return lax.dot_general(former, latter, (((0,), (0,)), ((), ())), preferred_element_type=jnp.float32)

def outer_cols(former, latter):
    return lax.dot_general(former, latter, (((1,), (1,)), ((), ())), preferred_element_type=jnp.float32)

def encode(rows_in, gain_vec, matrices, pieces):
    w_query, w_key, w_value, w_output = matrices
    x_float = rows_in.astype(jnp.float32)
    inv_rms = lax.rsqrt(lax.optimization_barrier(jnp.mean(x_float * x_float, axis=-1, keepdims=True)) + EPS)
    normed = (x_float * inv_rms * gain_vec).astype(jnp.bfloat16)
    layout = (pieces, R, EHEADS, EHD)
    queries = matmul(normed, w_query).astype(jnp.bfloat16).reshape(layout)
    keys_all = matmul(normed, w_key).astype(jnp.bfloat16).reshape(layout)
    values_all = matmul(normed, w_value).astype(jnp.bfloat16).reshape(layout)
    scores = batched('nqhd,nkhd->nhqk', queries, keys_all) * EHD ** (-0.5)
    soft_max = jax.nn.softmax(scores, axis=-1)
    soft_low = soft_max.astype(jnp.bfloat16)
    context = batched('nhqk,nkhd->nqhd', soft_low, values_all).astype(jnp.bfloat16).reshape(pieces * R, DE)
    encoded = (x_float + matmul(context, w_output)).astype(jnp.bfloat16)
    return (encoded, (x_float, inv_rms, normed, queries, keys_all, values_all, soft_max, soft_low, context))

def encode_backward(cotangent, saved, matrices, gain_vec, pieces):
    w_query, w_key, w_value, w_output = matrices
    x_float, inv_rms, normed, queries, keys_all, values_all, soft_max, soft_low, context = saved
    layout = (pieces, R, EHEADS, EHD)
    grad_output = inner_rows(context, cotangent)
    d_context = outer_cols(cotangent, w_output).astype(jnp.bfloat16).reshape(layout)
    d_soft = batched('nqhd,nkhd->nhqk', d_context, values_all)
    d_values = batched('nhqk,nqhd->nkhd', soft_low, d_context).astype(jnp.bfloat16).reshape(pieces * R, DE)
    d_scores = (soft_max * (d_soft - lax.optimization_barrier(jnp.sum(d_soft * soft_max, axis=-1, keepdims=True))) * EHD ** (-0.5)).astype(jnp.bfloat16)
    d_queries = batched('nhqk,nkhd->nqhd', d_scores, keys_all).astype(jnp.bfloat16).reshape(pieces * R, DE)
    d_keys = batched('nhqk,nqhd->nkhd', d_scores, queries).astype(jnp.bfloat16).reshape(pieces * R, DE)
    grad_query = inner_rows(normed, d_queries)
    grad_key = inner_rows(normed, d_keys)
    grad_value = inner_rows(normed, d_values)
    d_normed = outer_cols(d_queries, w_query) + outer_cols(d_keys, w_key) + outer_cols(d_values, w_value)
    scaled = d_normed * gain_vec
    d_rows = inv_rms * scaled - x_float * inv_rms ** 3 * lax.optimization_barrier(jnp.mean(x_float * scaled, axis=-1, keepdims=True))
    d_input = (cotangent.astype(jnp.float32) + d_rows).astype(jnp.bfloat16)
    return (d_input, (grad_query, grad_key, grad_value, grad_output))

def attend(grouped, pairs):
    group_count, span_rows, width_here = grouped.shape
    heads_here = width_here // HD
    key_rows = pairs.shape[1]
    split_q = grouped.reshape(group_count, span_rows, heads_here, HD)
    split_k = pairs[..., :width_here].reshape(group_count, key_rows, heads_here, HD)
    split_v = pairs[..., width_here:].reshape(group_count, key_rows, heads_here, HD)
    scores = batched('gqhd,gkhd->ghqk', split_q, split_k) * HD ** (-0.5)
    soft_max = jax.nn.softmax(scores, axis=-1)
    soft_low = soft_max.astype(jnp.bfloat16)
    return batched('ghqk,gkhd->gqhd', soft_low, split_v).astype(jnp.bfloat16).reshape(group_count * span_rows, width_here)

def reference(hidden, dec_gain, cca_query, cca_key, cca_value, cca_out, neighbours, enc_gain, enc_query, enc_key, enc_value, enc_output, enc_cotangent, neighbour_ids):
    pieces = COLUMNS * CH_DEV * K
    matrices = (enc_query, enc_key, enc_value, enc_output)
    encoded, saved = encode(neighbours.reshape(pieces * R, DE), enc_gain, matrices, pieces)
    d_input, partials = encode_backward(enc_cotangent.reshape(pieces * R, DE), saved, matrices, enc_gain, pieces)
    grads = tuple((partial_sum / pieces for partial_sum in partials))
    groups_all = encoded.reshape(COLUMNS, CH_DEV * K, R, DE)
    id_blocks = neighbour_ids.reshape(COLUMNS, CH_DEV, K).astype(jnp.int32)
    last_rows = jax.vmap(lambda group_rows, chosen: jnp.take(group_rows, chosen, axis=0))(groups_all, id_blocks[:, CH_DEV - 1, :])
    earlier_all = jnp.concatenate([jnp.zeros_like(last_rows[:1]), last_rows[:-1]], axis=0)
    pair_weight = jnp.concatenate([cca_key, cca_value], axis=1)
    blocks = hidden.reshape(COLUMNS, TOK_DEV, D)

    def one_column(packed):
        block_rows, column_rows, chosen, earlier, column_index = packed
        key_value = matmul(column_rows.reshape(CH_DEV * K * R, DE), pair_weight).astype(jnp.bfloat16).reshape(CH_DEV * K, R, 2 * D)
        own_pairs = jnp.take(key_value, chosen, axis=0).reshape(CH_DEV, K * R, 2 * D)
        before = matmul(earlier.reshape(K * R, DE), pair_weight).astype(jnp.bfloat16).reshape(1, K * R, 2 * D)
        groups = jnp.concatenate([before, own_pairs], axis=0)
        hidden_f = block_rows.astype(jnp.float32)
        inv_rms = lax.rsqrt(lax.optimization_barrier(jnp.mean(hidden_f * hidden_f, axis=-1, keepdims=True)) + EPS)
        normed = (hidden_f * inv_rms * dec_gain).astype(jnp.bfloat16)
        queries = matmul(normed, cca_query).astype(jnp.bfloat16)
        padded = jnp.concatenate([jnp.zeros((1, D), jnp.bfloat16), queries, jnp.zeros((C - 1, D), jnp.bfloat16)], axis=0).reshape(CH_DEV + 1, C, D)
        context = attend(padded, groups)[1:TOK_DEV + 1]
        position = (column_index * TOK_DEV + jnp.arange(TOK_DEV, dtype=jnp.int32) + C) % SEQ_LEN
        context = jnp.where((position >= C - 1)[:, None], context, jnp.zeros_like(context))
        return (hidden_f + matmul(context, cca_out)).astype(jnp.bfloat16)
    mixed = lax.map(one_column, (blocks, groups_all, id_blocks, earlier_all, jnp.arange(COLUMNS, dtype=jnp.int32)))
    return (mixed.reshape(TOKENS, D), d_input.reshape(neighbours.shape), grads[0], grads[1], grads[2], grads[3])
```

```python
import jax
import jax.numpy as jnp
from jax import lax
from jax.sharding import PartitionSpec as P

HD = 128
DE = 896
EHEADS = 14
EHD = 64
C = 64
R = 128
K = 2
SEQ_LEN = 2048


EPS = 1e-06


AXES = ("enc", "seq")
PLACES = [(x, y, z, c) for x in range(4) for y in range(4) for z in range(4) for c in range(2)]


def device_of(x, y, z, c):
    x, y, z = x % 4, y % 4, z % 4
    return ((y % 2) * 2 + c) * 32 + x * 8 + (y // 2) * 4 + z


def pairs_to(target):
    return [(device_of(*place), device_of(*target(*place))) for place in PLACES]


SIBLING = pairs_to(lambda x, y, z, c: (x, y, z, 1 - c))
PARTNER = pairs_to(lambda x, y, z, c: (x, y + 1 - 2 * (y % 2), z, c))
ACROSS_Y = pairs_to(lambda x, y, z, c: (x, y + 2 * c - 1, z, c))
FIRST = [pairs_to(lambda x, y, z, c, k=k: (x + k, y, z, c) if c == 0 else (x, y, z + k, c)) for k in range(4)]
SECOND = [pairs_to(lambda x, y, z, c, k=k: (x, y, z + k, c) if c == 0 else (x + k, y, z, c)) for k in range(4)]
THIRD = [pairs_to(lambda x, y, z, c, k=k: (x, y + k, z, c)) for k in range(4)]


def sent(x, pairs):
    return lax.ppermute(x, AXES, pairs)


def place():
    e, s = lax.axis_index("enc"), lax.axis_index("seq")
    return s // 8, 2 * ((s // 4) % 2) + e // 2, s % 4, e % 2


def gradient_row_order():
    x, y, z, c = place()
    i = jnp.arange(896, dtype=jnp.int32)
    half, i = i // 448, i % 448
    first, i = i // 112, i % 112
    second, i = i // 28, i % 28
    third, row = i // 7, i % 7
    core = jnp.where(half == 0, 1 - c, c)
    tx = (x + jnp.where(core == 0, first, second)) % 4
    tz = (z + jnp.where(core == 0, second, first)) % 4
    ty = (y + third) % 4
    return 7 * (((ty % 2) * 2 + core) * 32 + tx * 8 + (ty // 2) * 4 + tz) + row


def reduced_rows(kept, received):
    low = jnp.bfloat16
    total = kept.astype(jnp.float32) + received.astype(jnp.float32)
    for pairs in (FIRST, SECOND, THIRD):
        size = total.shape[0] // 4
        chunk = [total[k * size : (k + 1) * size] for k in range(4)]
        got = [sent(chunk[k].astype(low), pairs[k]).astype(jnp.float32) for k in (1, 3, 2)]
        total = chunk[0] + got[0] + got[1] + got[2]
    return total


def shifted(value, axis, steps):
    count = lax.axis_size(axis)
    initial, last = (max(0, -steps), min(count, count - steps))
    return lax.ppermute(value, axis, [(source, source + steps) for source in range(initial, last)])


def batched(pattern, former, latter):
    return jnp.einsum(pattern, former, latter, preferred_element_type=jnp.float32)


def matmul(former, latter):
    return jnp.dot(former, latter, preferred_element_type=jnp.float32)


def inner_rows(former, latter):
    return lax.dot_general(
        former, latter, (((0,), (0,)), ((), ())), preferred_element_type=jnp.float32
    )


def outer_cols(former, latter):
    return lax.dot_general(
        former, latter, (((1,), (1,)), ((), ())), preferred_element_type=jnp.float32
    )


def encode(rows_in, gain_vec, matrices, pieces):
    w_query, w_key, w_value, w_output = matrices
    x_float = rows_in.astype(jnp.float32)
    inv_rms = lax.rsqrt(jnp.mean(x_float * x_float, axis=-1, keepdims=True) + EPS)
    normed = (x_float * inv_rms * gain_vec).astype(jnp.bfloat16)
    layout = (pieces, R, EHEADS, EHD)
    queries = matmul(normed, w_query).astype(jnp.bfloat16).reshape(layout)
    keys_all = matmul(normed, w_key).astype(jnp.bfloat16).reshape(layout)
    values_all = matmul(normed, w_value).astype(jnp.bfloat16).reshape(layout)
    scores = batched("nqhd,nkhd->nhqk", queries, keys_all) * EHD ** (-0.5)
    soft_max = jax.nn.softmax(scores, axis=-1)
    soft_low = soft_max.astype(jnp.bfloat16)
    context = (
        batched("nhqk,nkhd->nqhd", soft_low, values_all)
        .astype(jnp.bfloat16)
        .reshape(pieces * R, DE)
    )
    encoded = (x_float + matmul(context, w_output)).astype(jnp.bfloat16)
    return (
        encoded,
        (x_float, inv_rms, normed, queries, keys_all, values_all, soft_max, soft_low, context),
    )


def encode_backward(cotangent, saved, matrices, gain_vec, pieces):
    w_query, w_key, w_value, w_output = matrices
    x_float, inv_rms, normed, queries, keys_all, values_all, soft_max, soft_low, context = saved
    layout = (pieces, R, EHEADS, EHD)
    d_context = outer_cols(cotangent, w_output).astype(jnp.bfloat16).reshape(layout)
    d_soft = batched("nqhd,nkhd->nhqk", d_context, values_all)
    d_values = (
        batched("nhqk,nqhd->nkhd", soft_low, d_context).astype(jnp.bfloat16).reshape(pieces * R, DE)
    )
    d_scores = (
        soft_max * (d_soft - jnp.sum(d_soft * soft_max, axis=-1, keepdims=True)) * EHD ** (-0.5)
    ).astype(jnp.bfloat16)
    d_queries = (
        batched("nhqk,nkhd->nqhd", d_scores, keys_all).astype(jnp.bfloat16).reshape(pieces * R, DE)
    )
    d_keys = (
        batched("nhqk,nqhd->nkhd", d_scores, queries).astype(jnp.bfloat16).reshape(pieces * R, DE)
    )
    order = gradient_row_order()
    picks = (order[:, None] == jnp.arange(DE, dtype=jnp.int32)[None, :]).astype(jnp.bfloat16)
    normed_t = outer_cols(picks, normed).astype(jnp.bfloat16)
    context_t = outer_cols(picks, context).astype(jnp.bfloat16)
    partials = jnp.concatenate(
        [matmul(normed_t, d).astype(jnp.bfloat16) for d in (d_queries, d_keys, d_values)]
        + [matmul(context_t, cotangent).astype(jnp.bfloat16)],
        axis=1,
    )
    d_normed = (
        outer_cols(d_queries, w_query) + outer_cols(d_keys, w_key) + outer_cols(d_values, w_value)
    )
    scaled = d_normed * gain_vec
    d_rows = inv_rms * scaled - x_float * inv_rms**3 * jnp.mean(
        x_float * scaled, axis=-1, keepdims=True
    )
    d_input = (cotangent.astype(jnp.float32) + d_rows).astype(jnp.bfloat16)
    return (d_input, partials)


def attend(grouped, pairs):
    group_count, span_rows, width_here = grouped.shape
    heads_here = width_here // HD
    key_rows = pairs.shape[1]
    split_q = grouped.reshape(group_count, span_rows, heads_here, HD)
    split_k = pairs[..., :width_here].reshape(group_count, key_rows, heads_here, HD)
    split_v = pairs[..., width_here:].reshape(group_count, key_rows, heads_here, HD)
    scores = batched("gqhd,gkhd->ghqk", split_q, split_k) * HD ** (-0.5)
    soft_max = jax.nn.softmax(scores, axis=-1)
    soft_low = soft_max.astype(jnp.bfloat16)
    return (
        batched("ghqk,gkhd->gqhd", soft_low, split_v)
        .astype(jnp.bfloat16)
        .reshape(group_count * span_rows, width_here)
    )


def on_device(
    hidden,
    dec_gain,
    cca_query,
    cca_key,
    cca_value,
    cca_out,
    neighbours,
    enc_gain,
    enc_query,
    enc_key,
    enc_value,
    enc_output,
    enc_cotangent,
    neighbour_ids,
):
    enc_index = lax.axis_index("enc")
    own = jnp.concatenate([enc_query, enc_key, enc_value, enc_output], axis=1)
    from_sibling, far = sent(own, SIBLING), sent(own, ACROSS_Y)
    shards = jnp.stack([own, from_sibling, far, sent(far, SIBLING)])
    joined = jnp.concatenate(
        [lax.dynamic_index_in_dim(shards, enc_index ^ r, 0, keepdims=False) for r in range(4)], axis=0
    )
    matrices = tuple(joined[:, k * DE : (k + 1) * DE] for k in range(4))
    local_count = neighbours.shape[1]
    encoded, saved = encode(
        neighbours.reshape(local_count * R, DE), enc_gain, matrices, local_count
    )
    d_input, partials = encode_backward(
        enc_cotangent.reshape(local_count * R, DE), saved, matrices, enc_gain, local_count
    )
    pool_total = local_count * lax.axis_size("enc") * lax.axis_size("seq")
    received = sent(partials[:448], SIBLING)
    rows = reduced_rows(partials[448:], received) / pool_total
    grads = tuple(rows[:, k * DE : (k + 1) * DE] for k in range(4))
    head_width = cca_key.shape[1]
    encoded_nb = encoded.reshape(local_count, R, DE)
    pair_weight = jnp.concatenate([cca_key, cca_value], axis=1)
    pair_own = jnp.concatenate([encoded_nb, sent(encoded_nb, SIBLING)], axis=0)
    far_nb = sent(encoded_nb, PARTNER)
    all_nb = jnp.concatenate([pair_own, far_nb, sent(far_nb, SIBLING)], axis=0)
    key_value = batched("nrd,de->nre", all_nb, pair_weight).astype(jnp.bfloat16)
    stretch_count = neighbour_ids.shape[0]
    own_pairs = jnp.take(key_value, neighbour_ids ^ (2 * enc_index), axis=0).reshape(
        stretch_count, K * R, 2 * head_width
    )
    hidden_f = hidden.astype(jnp.float32)
    inv_rms = lax.rsqrt(jnp.mean(hidden_f * hidden_f, axis=-1, keepdims=True) + EPS)
    normed = (hidden_f * inv_rms * dec_gain).astype(jnp.bfloat16)
    queries = matmul(normed, cca_query).astype(jnp.bfloat16)
    token_count = hidden.shape[0]
    incoming = shifted(queries[: C - 1], "seq", -1)
    own_groups = jnp.concatenate([queries[C - 1 :], incoming], axis=0).reshape(
        stretch_count, C, head_width
    )
    own_context = attend(own_groups, own_pairs)
    returned = shifted(own_context[token_count - (C - 1) :], "seq", 1)
    context = jnp.concatenate([returned, own_context[: token_count - (C - 1)]], axis=0)
    position = (
        lax.axis_index("seq") * token_count + jnp.arange(token_count, dtype=jnp.int32) + C
    ) % SEQ_LEN
    context = jnp.where((position >= C - 1)[:, None], context, jnp.zeros_like(context))
    partial_out = matmul(context, cca_out)
    width = partial_out.shape[1] // 4
    block = [
        lax.dynamic_slice_in_dim(partial_out, (enc_index ^ r) * width, width, 1) for r in range(4)
    ]
    low, wide = jnp.bfloat16, jnp.float32
    got3 = sent(block[3].astype(low), SIBLING).astype(wide)
    got2 = sent((block[2] + got3).astype(low), PARTNER).astype(wide)
    got1 = sent(block[1].astype(low), SIBLING).astype(wide)
    branch = block[0] + got1 + got2
    slice_width = branch.shape[1]
    residual = lax.dynamic_slice_in_dim(
        hidden_f, lax.axis_index("enc") * slice_width, slice_width, 1
    )
    mixed = (residual + branch).astype(jnp.bfloat16)
    return (mixed, d_input.reshape(neighbours.shape), grads[0], grads[1], grads[2], grads[3])


def solution(mesh):
    return jax.shard_map(
        on_device,
        mesh=mesh,
        in_specs=(
            P("seq", None),
            P(),
            P(None, "enc"),
            P(None, "enc"),
            P(None, "enc"),
            P("enc", None),
            P("seq", "enc", None, None),
            P(),
            P("enc", None),
            P("enc", None),
            P("enc", None),
            P("enc", None),
            P("seq", "enc", None, None),
            P("seq", None),
        ),
        out_specs=(
            P("seq", "enc"),
            P("seq", "enc", None, None),
            P(("enc", "seq"), None),
            P(("enc", "seq"), None),
            P(("enc", "seq"), None),
            P(("enc", "seq"), None),
        ),
        check_vma=False,
    )
```

```python
import jax
import jax.numpy as jnp
from jax import lax
from jax.experimental import pallas as pl
from jax.experimental.pallas import tpu as pltpu
from jax.sharding import PartitionSpec as P

HD = 128
DE = 896
EHEADS = 14
EHD = 64
C = 64
R = 128
K = 2
SEQ_LEN = 2048


EPS = 1e-06


AXES = ("enc", "seq")
PLACES = [(x, y, z, c) for x in range(4) for y in range(4) for z in range(4) for c in range(2)]


def device_of(x, y, z, c):
    x, y, z = x % 4, y % 4, z % 4
    return ((y % 2) * 2 + c) * 32 + x * 8 + (y // 2) * 4 + z


def pairs_to(target):
    return [(device_of(*place), device_of(*target(*place))) for place in PLACES]


SIBLING = pairs_to(lambda x, y, z, c: (x, y, z, 1 - c))
PARTNER = pairs_to(lambda x, y, z, c: (x, y + 1 - 2 * (y % 2), z, c))
ACROSS_Y = pairs_to(lambda x, y, z, c: (x, y + 2 * c - 1, z, c))
FIRST = [pairs_to(lambda x, y, z, c, k=k: (x + k, y, z, c) if c == 0 else (x, y, z + k, c)) for k in range(4)]
SECOND = [pairs_to(lambda x, y, z, c, k=k: (x, y, z + k, c) if c == 0 else (x + k, y, z, c)) for k in range(4)]
THIRD = [pairs_to(lambda x, y, z, c, k=k: (x, y + k, z, c)) for k in range(4)]


def sent(x, pairs):
    return lax.ppermute(x, AXES, pairs)


def place():
    e, s = lax.axis_index("enc"), lax.axis_index("seq")
    return s // 8, 2 * ((s // 4) % 2) + e // 2, s % 4, e % 2


def gradient_row_order():
    x, y, z, c = place()
    i = jnp.arange(896, dtype=jnp.int32)
    half, i = i // 448, i % 448
    first, i = i // 112, i % 112
    second, i = i // 28, i % 28
    third, row = i // 7, i % 7
    core = jnp.where(half == 0, 1 - c, c)
    tx = (x + jnp.where(core == 0, first, second)) % 4
    tz = (z + jnp.where(core == 0, second, first)) % 4
    ty = (y + third) % 4
    return 7 * (((ty % 2) * 2 + core) * 32 + tx * 8 + (ty // 2) * 4 + tz) + row


def reduced_rows(kept, received):
    low = jnp.bfloat16
    total = kept.astype(jnp.float32) + received.astype(jnp.float32)
    for pairs in (FIRST, SECOND, THIRD):
        size = total.shape[0] // 4
        chunk = [total[k * size : (k + 1) * size] for k in range(4)]
        got = [sent(chunk[k].astype(low), pairs[k]).astype(jnp.float32) for k in (1, 3, 2)]
        total = chunk[0] + got[0] + got[1] + got[2]
    return total


def shifted(value, axis, steps):
    count = lax.axis_size(axis)
    initial, last = (max(0, -steps), min(count, count - steps))
    return lax.ppermute(value, axis, [(source, source + steps) for source in range(initial, last)])


LOW, WIDE = jnp.bfloat16, jnp.float32
ROWS = 256
PAIRS = EHEADS // 2
VM = pl.BlockSpec(memory_space=pltpu.VMEM)
SM = pl.BlockSpec(memory_space=pltpu.SMEM)


def shape(dims, kind=LOW):
    return jax.ShapeDtypeStruct(dims, kind)


def nn(a, b):
    return lax.dot_general(a, b, (((1,), (0,)), ((), ())), preferred_element_type=WIDE)


def nt(a, b):
    return lax.dot_general(a, b, (((1,), (1,)), ((), ())), preferred_element_type=WIDE)


def tn(a, b):
    return lax.dot_general(a, b, (((0,), (0,)), ((), ())), preferred_element_type=WIDE)


def cost(flops, nbytes):
    return pl.CostEstimate(flops=int(flops), transcendentals=0, bytes_accessed=int(nbytes))


def two_heads(x):
    lane = lax.broadcasted_iota(jnp.int32, x.shape, 1)
    zero = jnp.zeros_like(x)
    return jnp.concatenate([jnp.where(lane < EHD, x, zero), jnp.where(lane < EHD, zero, x)], axis=0)


def one_pair(x):
    lane = lax.broadcasted_iota(jnp.int32, (R, 2 * EHD), 1)
    return jnp.where(lane < EHD, x[:R], x[R:])


def encode_kernel(e_ref, x_ref, gain_ref, *refs):
    shards = refs[:16]
    enc_ref, norm_ref, q_ref, k_ref, v_ref, ctx_ref, p_ref, w_ref = refs[16:]
    for r in range(4):
        at = pl.ds(pl.multiple_of((e_ref[0] ^ r) * 224, 16), 224)
        for m in range(4):
            w_ref[at, m * DE : (m + 1) * DE] = shards[4 * r + m][...]
    x = x_ref[...].astype(WIDE)
    inv = lax.rsqrt(jnp.mean(x * x, axis=-1, keepdims=True) + EPS)
    norm_ref[...] = (x * inv * gain_ref[...]).astype(LOW)
    for m, out in enumerate((q_ref, k_ref, v_ref)):
        out[...] = nn(norm_ref[...], w_ref[:, m * DE : (m + 1) * DE]).astype(LOW)

    @pl.loop(0, 2 * PAIRS, unroll=2)
    def _(i):
        n, pair = i // PAIRS, i % PAIRS
        at = (pl.ds(pl.multiple_of(n * R, R), R), pl.ds(pl.multiple_of(pair * 2 * EHD, 2 * EHD), 2 * EHD))
        s = nt(two_heads(q_ref[at]), k_ref[at]) * EHD ** (-0.5)
        ex = jnp.exp(s - jnp.max(s, axis=-1, keepdims=True))
        p = ex * (1.0 / jnp.sum(ex, axis=-1, keepdims=True))
        p_ref[i] = p
        ctx_ref[at] = one_pair(nn(p.astype(LOW), v_ref[at])).astype(LOW)

    enc_ref[...] = (x_ref[...].astype(WIDE) + nn(ctx_ref[...], w_ref[:, 3 * DE :])).astype(LOW)


def encode(e, x, gain, shards):
    big = ROWS * DE * 2
    return pl.pallas_call(
        encode_kernel,
        out_shape=[shape((ROWS, DE))] * 6 + [shape((2 * PAIRS, 2 * R, R), WIDE), shape((DE, 4 * DE))],
        in_specs=[SM] + [VM] * 18,
        out_specs=[VM] * 8,
        cost_estimate=cost(2.2e9, 12 * big),
        name="encode",
    )(e, x, gain, *shards)


def backward_kernel(cot_ref, norm_ref, q_ref, k_ref, v_ref, ctx_ref, p_ref, w_ref, order_ref, d_ref, g_ref, nt_ref, ct_ref, dctx_ref):
    dctx_ref[...] = nt(cot_ref[...], w_ref[:, 3 * DE :]).astype(LOW)

    @pl.loop(0, 2 * PAIRS, unroll=2)
    def _(i):
        n, pair = i // PAIRS, i % PAIRS
        rows = pl.ds(pl.multiple_of(n * R, R), R)
        col = pair * 2 * EHD
        at = (rows, pl.ds(pl.multiple_of(col, 2 * EHD), 2 * EHD))
        d2, q2 = two_heads(dctx_ref[at]), two_heads(q_ref[at])
        p = p_ref[i]
        dp = nt(d2, v_ref[at])
        ds = (p * (dp - jnp.sum(dp * p, axis=-1, keepdims=True)) * EHD ** (-0.5)).astype(LOW)
        for m, value in enumerate((one_pair(nn(ds, k_ref[at])), tn(ds, q2), tn(p.astype(LOW), d2))):
            d_ref[rows, pl.ds(pl.multiple_of(m * DE + col, 2 * EHD), 2 * EHD)] = value.astype(LOW)

    half = DE // 2
    for h in range(2):
        rows = slice(h * half, (h + 1) * half)
        spot = lax.broadcasted_iota(jnp.int32, (half, DE), 1)
        picks = (order_ref[rows, :] == spot).astype(WIDE).astype(LOW)
        nt_ref[rows, :] = nt(picks, norm_ref[...]).astype(LOW)
        ct_ref[rows, :] = nt(picks, ctx_ref[...]).astype(LOW)
    gradient_rows(nt_ref, ct_ref, d_ref, cot_ref, g_ref, 0)


def gradient_rows(nt_ref, ct_ref, d_ref, cot_ref, g_ref, start):
    @pl.loop(0, 2)
    def _(i):
        into = pl.ds(pl.multiple_of(i * 224, 16), 224)
        rows = pl.ds(pl.multiple_of(start + i * 224, 16), 224)
        for m in range(3):
            cols = slice(m * DE, (m + 1) * DE)
            g_ref[into, cols] = nn(nt_ref[rows, :], d_ref[:, cols]).astype(LOW)
        g_ref[into, 3 * DE :] = nn(ct_ref[rows, :], cot_ref[...]).astype(LOW)


def backward(cot, saved, w, order):
    norm, q, k, v, ctx, p = saved
    return pl.pallas_call(
        backward_kernel,
        out_shape=[shape((ROWS, 3 * DE)), shape((DE // 2, 4 * DE)), shape((DE, ROWS)), shape((DE, ROWS))],
        in_specs=[VM] * 9,
        out_specs=[VM] * 4,
        scratch_shapes=[pltpu.VMEM((ROWS, DE), LOW)],
        cost_estimate=cost(3e9, 12 * ROWS * DE * 2),
        name="backward",
    )(cot, norm, q, k, v, ctx, p, w, order)


def finish_kernel(x_ref, gain_ref, cot_ref, d_ref, w_ref, nt_ref, ct_ref, dx_ref, g_ref, s_ref):
    gradient_rows(nt_ref, ct_ref, d_ref, cot_ref, g_ref, DE // 2)
    for c0 in range(0, DE, 256):
        c1 = min(c0 + 256, DE)
        s_ref[:, c0:c1] = nt(d_ref[...], w_ref[c0:c1, : 3 * DE])
    x = x_ref[...].astype(WIDE)
    inv = lax.rsqrt(jnp.mean(x * x, axis=-1, keepdims=True) + EPS)
    scaled = s_ref[...] * gain_ref[...]
    inner = jnp.mean(x * scaled, axis=-1, keepdims=True)
    dx_ref[...] = (cot_ref[...].astype(WIDE) + inv * scaled - x * (inv * inv * inv * inner)).astype(LOW)


def finish(x, gain, cot, d, w, norm_t, ctx_t):
    return pl.pallas_call(
        finish_kernel,
        out_shape=[shape((ROWS, DE)), shape((DE // 2, 4 * DE))],
        in_specs=[VM] * 7,
        out_specs=[VM] * 2,
        scratch_shapes=[pltpu.VMEM((ROWS, DE), WIDE)],
        cost_estimate=cost(2.1e9, 12 * ROWS * DE * 2),
        name="finish",
    )(x, gain, cot, d, w, norm_t, ctx_t)


def attend_kernel(info_ref, n0, n1, n2, n3, q_ref, qin_ref, wk_ref, wv_ref, ctx_ref, send_ref, kf, vf, qf, of):
    for r, block in enumerate((n0, n1, n2, n3)):
        kf[r * ROWS : (r + 1) * ROWS, :] = nn(block[...], wk_ref[...]).astype(LOW)
        vf[r * ROWS : (r + 1) * ROWS, :] = nn(block[...], wv_ref[...]).astype(LOW)
    qf[:ROWS, :] = q_ref[...].astype(WIDE)
    qf[ROWS:, :] = qin_ref[...].astype(WIDE)
    of[...] = jnp.zeros_like(of)
    for u in range(4):
        lo = C - 1 + C * u
        q = qf[lo : lo + C, :].astype(LOW)
        first = pl.ds(pl.multiple_of(info_ref[2 * u] * R, R), R)
        second = pl.ds(pl.multiple_of(info_ref[2 * u + 1] * R, R), R)
        for h in range(2):
            cols = slice(h * HD, (h + 1) * HD)
            s0 = nt(q[:, cols], kf[first, cols]) * HD ** (-0.5)
            s1 = nt(q[:, cols], kf[second, cols]) * HD ** (-0.5)
            top = jnp.maximum(jnp.max(s0, axis=-1, keepdims=True), jnp.max(s1, axis=-1, keepdims=True))
            e0, e1 = jnp.exp(s0 - top), jnp.exp(s1 - top)
            scale = 1.0 / (jnp.sum(e0, axis=-1, keepdims=True) + jnp.sum(e1, axis=-1, keepdims=True))
            out = nn((e0 * scale).astype(LOW), vf[first, cols]) + nn((e1 * scale).astype(LOW), vf[second, cols])
            of[lo : lo + C, cols] = out
    token = lax.broadcasted_iota(jnp.int32, (ROWS, 2 * HD), 0)
    position = (info_ref[8] * ROWS + token + C) & (SEQ_LEN - 1)
    ctx_ref[...] = jnp.where(position >= C - 1, of[:ROWS, :], 0.0).astype(LOW)
    send_ref[...] = of[ROWS:, :].astype(LOW)


def attend(info, blocks, q, q_in, wk, wv):
    width = q.shape[1]
    whole = [pl.BlockSpec((ROWS, DE), lambda i: (0, 0))] * 4
    cols = lambda rows: pl.BlockSpec((rows, 2 * HD), lambda i: (0, i))
    return pl.pallas_call(
        attend_kernel,
        grid=(width // (2 * HD),),
        out_shape=[shape((ROWS, width)), shape((C, width))],
        in_specs=[SM] + whole + [cols(ROWS), cols(C), cols(DE), cols(DE)],
        out_specs=[cols(ROWS), cols(C)],
        scratch_shapes=[
            pltpu.VMEM((4 * ROWS, 2 * HD), LOW),
            pltpu.VMEM((4 * ROWS, 2 * HD), LOW),
            pltpu.VMEM((ROWS + C, 2 * HD), WIDE),
            pltpu.VMEM((ROWS + C, 2 * HD), WIDE),
        ],
        cost_estimate=cost(4.3e9, 6e6),
        name="attend",
    )(info, *blocks, q, q_in, wk, wv)


def project_kernel(e_ref, ctx_ref, ret_ref, w_ref, out_ref, full):
    @pl.when(pl.program_id(0) == 0)
    def _():
        full[...] = ctx_ref[...]
        full[:C, :] = ctx_ref[:C, :] + ret_ref[...]

    out_ref[...] = nn(full[...], w_ref[...]).astype(out_ref.dtype)


def project(e, ctx, returned, w, r, kind):
    width = ctx.shape[1]
    n = 2
    tile = width // n
    return pl.pallas_call(
        project_kernel,
        grid_spec=pltpu.PrefetchScalarGridSpec(
            num_scalar_prefetch=1,
            grid=(n,),
            in_specs=[
                pl.BlockSpec((ROWS, width), lambda i, e: (0, 0)),
                pl.BlockSpec((C, width), lambda i, e: (0, 0)),
                pl.BlockSpec((width, tile), lambda i, e: (0, (e[0] ^ r) * n + i)),
            ],
            out_specs=pl.BlockSpec((ROWS, tile), lambda i, e: (0, i)),
            scratch_shapes=[pltpu.VMEM((ROWS, width), LOW)],
        ),
        out_shape=shape((ROWS, width), kind),
        cost_estimate=cost(5.4e8, 3e6),
        name=f"project_{r}",
    )(e, ctx, returned, w)


def total_kernel(e_ref, hidden_ref, a_ref, b_ref, c_ref, out_ref):
    branch = a_ref[...] + b_ref[...].astype(WIDE) + c_ref[...].astype(WIDE)
    out_ref[...] = (hidden_ref[...].astype(WIDE) + branch).astype(LOW)


def total(e, hidden, a, b, c):
    width = a.shape[1]
    flat = pl.BlockSpec((ROWS, width), lambda i, e: (0, 0))
    return pl.pallas_call(
        total_kernel,
        grid_spec=pltpu.PrefetchScalarGridSpec(
            num_scalar_prefetch=1,
            grid=(1,),
            in_specs=[pl.BlockSpec((ROWS, width), lambda i, e: (0, e[0])), flat, flat, flat],
            out_specs=flat,
        ),
        out_shape=shape((ROWS, width)),
        cost_estimate=cost(1e6, 3e6),
        name="total",
    )(e, hidden, a, b, c)


def on_device(
    hidden,
    dec_gain,
    cca_query,
    cca_key,
    cca_value,
    cca_out,
    neighbours,
    enc_gain,
    enc_query,
    enc_key,
    enc_value,
    enc_output,
    enc_cotangent,
    neighbour_ids,
):
    enc_index, seq_index = lax.axis_index("enc"), lax.axis_index("seq")
    e = enc_index.astype(jnp.int32).reshape(1)
    own = (enc_query, enc_key, enc_value, enc_output)
    far = [sent(m, ACROSS_Y) for m in own]
    near = [sent(m, SIBLING) for m in own]
    far_near = [sent(m, SIBLING) for m in far]

    hidden_f = hidden.astype(WIDE)
    inv_rms = lax.rsqrt(jnp.mean(hidden_f * hidden_f, axis=-1, keepdims=True) + EPS)
    normed = (hidden_f * inv_rms * dec_gain).astype(LOW)
    queries = jnp.dot(normed, cca_query, preferred_element_type=WIDE).astype(LOW)
    q_in = shifted(queries[:C], "seq", -1)

    x = neighbours.reshape(ROWS, DE)
    cot = enc_cotangent.reshape(ROWS, DE)
    gain = enc_gain.reshape(1, DE)
    encoded, *saved, w = encode(e, x, gain, (*own, *near, *far, *far_near))
    far_nb = sent(encoded, PARTNER)
    near_nb = sent(encoded, SIBLING)
    d, g_other, norm_t, ctx_t = backward(cot, saved, w, gradient_row_order().reshape(DE, 1))
    received = sent(g_other, SIBLING)
    far_near_nb = sent(far_nb, SIBLING)
    d_input, g_own = finish(x, gain, cot, d, w, norm_t, ctx_t)

    ids = (neighbour_ids ^ (2 * enc_index)).astype(jnp.int32).reshape(-1)
    info = jnp.concatenate([ids, seq_index.astype(jnp.int32).reshape(1)])
    context, to_next = attend(info, (encoded, near_nb, far_nb, far_near_nb), queries, q_in, cca_key, cca_value)
    returned = shifted(to_next, "seq", 1)

    got3 = sent(project(e, context, returned, cca_out, 3, LOW), SIBLING)
    part2 = project(e, context, returned, cca_out, 2, WIDE)
    got2 = sent((part2 + got3.astype(WIDE)).astype(LOW), PARTNER)
    got1 = sent(project(e, context, returned, cca_out, 1, LOW), SIBLING)
    part0 = project(e, context, returned, cca_out, 0, WIDE)

    pool_total = 2 * lax.axis_size("enc") * lax.axis_size("seq")
    rows = reduced_rows(g_own, received) / pool_total
    grads = tuple(rows[:, k * DE : (k + 1) * DE] for k in range(4))
    mixed = total(e, hidden, part0, got1, got2)
    return (mixed, d_input.reshape(neighbours.shape), grads[0], grads[1], grads[2], grads[3])


def solution(mesh):
    return jax.shard_map(
        on_device,
        mesh=mesh,
        in_specs=(
            P("seq", None),
            P(),
            P(None, "enc"),
            P(None, "enc"),
            P(None, "enc"),
            P("enc", None),
            P("seq", "enc", None, None),
            P(),
            P("enc", None),
            P("enc", None),
            P("enc", None),
            P("enc", None),
            P("seq", "enc", None, None),
            P("seq", None),
        ),
        out_specs=(
            P("seq", "enc"),
            P("seq", "enc", None, None),
            P(("enc", "seq"), None),
            P(("enc", "seq"), None),
            P(("enc", "seq"), None),
            P(("enc", "seq"), None),
        ),
        check_vma=False,
    )
```

```python
import functools

import jax
import jax.numpy as jnp
from jax import lax
from jax.experimental import pallas as pl
from jax.experimental.pallas import tpu as pltpu
from jax.sharding import PartitionSpec as P


HD = 128
DE = 896
EHEADS = 14
EHD = 64
C = 64
R = 128
SEQ_LEN = 2048


EPS = 1e-06


AXES = ("enc", "seq")
PLACES = [(x, y, z, c) for x in range(4) for y in range(4) for z in range(4) for c in range(2)]


def device_of(x, y, z, c):
    x, y, z = x % 4, y % 4, z % 4
    return ((y % 2) * 2 + c) * 32 + x * 8 + (y // 2) * 4 + z


def pairs_to(target):
    return [(device_of(*place), device_of(*target(*place))) for place in PLACES]


SIBLING = pairs_to(lambda x, y, z, c: (x, y, z, 1 - c))
PARTNER = pairs_to(lambda x, y, z, c: (x, y + 1 - 2 * (y % 2), z, c))
ACROSS_Y = pairs_to(lambda x, y, z, c: (x, y + 2 * c - 1, z, c))
FIRST = [pairs_to(lambda x, y, z, c, k=k: (x + k, y, z, c) if c == 0 else (x, y, z + k, c)) for k in range(4)]
SECOND = [pairs_to(lambda x, y, z, c, k=k: (x, y, z + k, c) if c == 0 else (x + k, y, z, c)) for k in range(4)]
THIRD = [pairs_to(lambda x, y, z, c, k=k: (x, y + k, z, c)) for k in range(4)]


def sent(x, pairs):
    return lax.ppermute(x, AXES, pairs)


def place():
    e, s = lax.axis_index("enc"), lax.axis_index("seq")
    return s // 8, 2 * ((s // 4) % 2) + e // 2, s % 4, e % 2


def gradient_row_order():
    x, y, z, c = place()
    i = jnp.arange(896, dtype=jnp.int32)
    half, i = i // 448, i % 448
    first, i = i // 112, i % 112
    second, i = i // 28, i % 28
    third, row = i // 7, i % 7
    core = jnp.where(half == 0, 1 - c, c)
    tx = (x + jnp.where(core == 0, first, second)) % 4
    tz = (z + jnp.where(core == 0, second, first)) % 4
    ty = (y + third) % 4
    return 7 * (((ty % 2) * 2 + core) * 32 + tx * 8 + (ty // 2) * 4 + tz) + row


def shifted(value, axis, steps):
    count = lax.axis_size(axis)
    initial, last = (max(0, -steps), min(count, count - steps))
    return lax.ppermute(value, axis, [(source, source + steps) for source in range(initial, last)])


LOW, WIDE = jnp.bfloat16, jnp.float32
ROWS = 256
PAIRS = EHEADS // 2
VM = pl.BlockSpec(memory_space=pltpu.VMEM)
ANY = pl.BlockSpec(memory_space=pl.ANY)
SM = pl.BlockSpec(memory_space=pltpu.SMEM)


def shape(dims, kind=LOW):
    return jax.ShapeDtypeStruct(dims, kind)


def nn(a, b):
    return lax.dot_general(a, b, (((1,), (0,)), ((), ())), preferred_element_type=WIDE)


def nt(a, b):
    return lax.dot_general(a, b, (((1,), (1,)), ((), ())), preferred_element_type=WIDE)


def tn(a, b):
    return lax.dot_general(a, b, (((0,), (0,)), ((), ())), preferred_element_type=WIDE)


def cost(flops, nbytes):
    return pl.CostEstimate(flops=int(flops), transcendentals=0, bytes_accessed=int(nbytes))


def two_heads(x):
    lane = lax.broadcasted_iota(jnp.int32, x.shape, 1)
    zero = jnp.zeros_like(x)
    return jnp.concatenate([jnp.where(lane < EHD, x, zero), jnp.where(lane < EHD, zero, x)], axis=0)


def one_pair(x):
    lane = lax.broadcasted_iota(jnp.int32, (R, 2 * EHD), 1)
    return jnp.where(lane < EHD, x[:R], x[R:])


def params(mib):
    return pltpu.CompilerParams(vmem_limit_bytes=mib << 20)


def joined(e_ref, shards, w_ref, count):
    for r in range(4):
        at = pl.ds(pl.multiple_of((e_ref[0] ^ r) * 224, 16), 224)
        for m in range(count):
            w_ref[at, m * DE : (m + 1) * DE] = shards[count * r + m][...]


def pair_at(i):
    n, pair = i // PAIRS, i % PAIRS
    return pl.ds(pl.multiple_of(n * R, R), R), pl.multiple_of(pair * 2 * EHD, 2 * EHD)


def queries_kernel(hidden_ref, gain_ref, w_ref, q_ref, norm):
    @pl.when(pl.program_id(0) == 0)
    def _():
        h = hidden_ref[...].astype(WIDE)
        inv = lax.rsqrt(jnp.mean(h * h, axis=-1, keepdims=True) + EPS)
        norm[...] = (h * inv * gain_ref[...][None, :]).astype(LOW)

    q_ref[...] = nn(norm[...], w_ref[...]).astype(LOW)


def query_projection(hidden, gain, w):
    rows, depth = hidden.shape
    tile = 256
    return pl.pallas_call(
        queries_kernel,
        grid=(w.shape[1] // tile,),
        out_shape=shape((rows, w.shape[1])),
        in_specs=[
            pl.BlockSpec((rows, depth), lambda i: (0, 0)),
            pl.BlockSpec((depth,), lambda i: (0,)),
            pl.BlockSpec((depth, tile), lambda i: (0, i)),
        ],
        out_specs=pl.BlockSpec((rows, tile), lambda i: (0, i)),
        scratch_shapes=[pltpu.VMEM((rows, depth), LOW)],
        compiler_params=params(20),
        cost_estimate=cost(2.2e9, 11e6),
        name="query_projection",
    )(hidden, gain, w)


def prep_kernel(x_ref, gain_ref, order_ref, norm_ref, picks_ref, nt_ref):
    x = x_ref[...].astype(WIDE)
    inv = lax.rsqrt(jnp.mean(x * x, axis=-1, keepdims=True) + EPS)
    norm_ref[...] = (x * inv * gain_ref[...][None, :]).astype(LOW)
    spot = lax.broadcasted_iota(jnp.int32, (DE, DE), 0)
    picks_ref[...] = (order_ref[...][None, :] == spot).astype(WIDE).astype(LOW)
    nt_ref[...] = nn(norm_ref[...], picks_ref[...]).T.astype(LOW)


def prepare(x, gain, order):
    return pl.pallas_call(
        prep_kernel,
        out_shape=[shape((ROWS, DE)), shape((DE, DE)), shape((DE, ROWS))],
        in_specs=[VM] * 3,
        out_specs=[VM] * 3,
        compiler_params=params(6),
        cost_estimate=cost(4.1e8, 3e6),
        name="prepare",
    )(x, gain, order)


def scores_kernel(e_ref, wait_ref, norm_ref, *refs):
    del wait_ref
    q_ref, k_ref, p_ref, w_ref = refs[8:]
    joined(e_ref, refs[:8], w_ref, 2)
    for m, out in enumerate((q_ref, k_ref)):
        out[...] = nn(norm_ref[...], w_ref[:, m * DE : (m + 1) * DE]).astype(LOW)

    @pl.loop(0, 2 * PAIRS, unroll=2)
    def _(i):
        rows, col = pair_at(i)
        at = (rows, pl.ds(col, 2 * EHD))
        s = nt(two_heads(q_ref[at]), k_ref[at]) * EHD ** (-0.5)
        ex = jnp.exp(s - jnp.max(s, axis=-1, keepdims=True))
        p_ref[i] = ex * (1.0 / jnp.sum(ex, axis=-1, keepdims=True))


def encode_scores(e, wait, norm, shards):
    return pl.pallas_call(
        scores_kernel,
        out_shape=[shape((ROWS, DE))] * 2 + [shape((2 * PAIRS, 2 * R, R), WIDE), shape((DE, 2 * DE))],
        in_specs=[SM, ANY] + [VM] * 9,
        out_specs=[VM] * 4,
        compiler_params=params(5),
        cost_estimate=cost(1.2e9, 6e6),
        name="encode_scores",
    )(e, wait, norm, *shards)


def values_kernel(e_ref, x_ref, norm_ref, p_ref, *refs):
    enc_ref, v_ref, ctx_ref, w_ref = refs[8:]
    joined(e_ref, refs[:8], w_ref, 2)
    v_ref[...] = nn(norm_ref[...], w_ref[:, :DE]).astype(LOW)

    @pl.loop(0, 2 * PAIRS, unroll=2)
    def _(i):
        rows, col = pair_at(i)
        at = (rows, pl.ds(col, 2 * EHD))
        ctx_ref[at] = one_pair(nn(p_ref[i].astype(LOW), v_ref[at])).astype(LOW)

    enc_ref[...] = (x_ref[...].astype(WIDE) + nn(ctx_ref[...], w_ref[:, DE:])).astype(LOW)


def encode_values(e, x, norm, p, shards):
    return pl.pallas_call(
        values_kernel,
        out_shape=[shape((ROWS, DE))] * 3 + [shape((DE, 2 * DE))],
        in_specs=[SM] + [VM] * 11,
        out_specs=[VM] * 4,
        compiler_params=params(4),
        cost_estimate=cost(1.2e9, 8e6),
        name="encode_values",
    )(e, x, norm, p, *shards)


def gradient_tile(nt_ref, ct_ref, d_ref, cot_ref, rows, m):
    if m == 3:
        return nn(ct_ref[rows, :], cot_ref[...])
    return nn(nt_ref[rows, :], d_ref[:, m * DE : (m + 1) * DE])


def backward_kernel(cot_ref, q_ref, k_ref, v_ref, ctx_ref, p_ref, w_ref, picks_ref, nt_ref, d_ref, g_ref, ct_ref, dctx_ref):
    dctx_ref[...] = nt(cot_ref[...], w_ref[:, DE:]).astype(LOW)

    @pl.loop(0, 2 * PAIRS, unroll=2)
    def _(i):
        rows, col = pair_at(i)
        at = (rows, pl.ds(col, 2 * EHD))
        d2, q2 = two_heads(dctx_ref[at]), two_heads(q_ref[at])
        p = p_ref[i]
        dp = nt(d2, v_ref[at])
        ds = (p * (dp - jnp.sum(dp * p, axis=-1, keepdims=True)) * EHD ** (-0.5)).astype(LOW)
        for m, value in enumerate((one_pair(nn(ds, k_ref[at])), tn(ds, q2), tn(p.astype(LOW), d2))):
            d_ref[rows, pl.ds(pl.multiple_of(m * DE + col, 2 * EHD), 2 * EHD)] = value.astype(LOW)

    ct_ref[...] = nn(ctx_ref[...], picks_ref[...]).T.astype(LOW)

    rows = slice(0, DE // 2)
    for m in range(4):
        g_ref[:, m * DE : (m + 1) * DE] = gradient_tile(nt_ref, ct_ref, d_ref, cot_ref, rows, m).astype(LOW)


def backward(cot, q, k, v, ctx, p, w_vo, picks, norm_t):
    return pl.pallas_call(
        backward_kernel,
        out_shape=[shape((ROWS, 3 * DE)), shape((DE // 2, 4 * DE)), shape((DE, ROWS))],
        in_specs=[VM] * 9,
        out_specs=[VM] * 3,
        scratch_shapes=[pltpu.VMEM((ROWS, DE), LOW)],
        compiler_params=params(6),
        cost_estimate=cost(2.6e9, 8e6),
        name="backward",
    )(cot, q, k, v, ctx, p, w_vo, picks, norm_t)


def finish_kernel(x_ref, gain_ref, cot_ref, d_ref, qk_ref, vo_ref, dx_ref, s_ref):
    for c0 in range(0, DE, 256):
        c1 = min(c0 + 256, DE)
        s_ref[:, c0:c1] = nt(d_ref[:, : 2 * DE], qk_ref[c0:c1, :]) + nt(d_ref[:, 2 * DE :], vo_ref[c0:c1, :DE])
    x = x_ref[...].astype(WIDE)
    inv = lax.rsqrt(jnp.mean(x * x, axis=-1, keepdims=True) + EPS)
    scaled = s_ref[...] * gain_ref[...][None, :]
    inner = jnp.mean(x * scaled, axis=-1, keepdims=True)
    dx_ref[...] = (cot_ref[...].astype(WIDE) + inv * scaled - x * (inv * inv * inv * inner)).astype(LOW)


def finish(x, gain, cot, d, w_qk, w_vo):
    return pl.pallas_call(
        finish_kernel,
        out_shape=shape((ROWS, DE)),
        in_specs=[VM] * 6,
        out_specs=VM,
        scratch_shapes=[pltpu.VMEM((ROWS, DE), WIDE)],
        compiler_params=params(5),
        cost_estimate=cost(1.3e9, 6e6),
        name="finish",
    )(x, gain, cot, d, w_qk, w_vo)


def own_kernel(nt_ref, ct_ref, d_ref, cot_ref, got_ref, own_ref, c1_ref, c2_ref, c3_ref):
    for k, out in enumerate((own_ref, c1_ref, c2_ref, c3_ref)):
        rows = slice(DE // 2 + 112 * k, DE // 2 + 112 * (k + 1))
        for m in range(4):
            cols = slice(m * DE, (m + 1) * DE)
            tile = gradient_tile(nt_ref, ct_ref, d_ref, cot_ref, rows, m)
            out[:, cols] = (tile + got_ref[112 * k : 112 * (k + 1), cols].astype(WIDE)).astype(out.dtype)


def own_gradients(norm_t, ctx_t, d, cot, got):
    return pl.pallas_call(
        own_kernel,
        out_shape=[shape((112, 4 * DE), WIDE)] + [shape((112, 4 * DE))] * 3,
        in_specs=[VM] * 5,
        out_specs=[VM] * 4,
        compiler_params=params(8),
        cost_estimate=cost(8.3e8, 8e6),
        name="own_gradients",
    )(norm_t, ctx_t, d, cot, got)


def pairs_kernel(n0, n1, n2, n3, wk_ref, wv_ref, k_ref, v_ref):
    @pl.loop(0, k_ref.shape[1] // 256)
    def _(i):
        cols = pl.ds(pl.multiple_of(i * 256, 256), 256)
        for r, block in enumerate((n0, n1, n2, n3)):
            k_ref[r * ROWS : (r + 1) * ROWS, cols] = nn(block[...], wk_ref[:, cols]).astype(LOW)
            v_ref[r * ROWS : (r + 1) * ROWS, cols] = nn(block[...], wv_ref[:, cols]).astype(LOW)


def pair_kv(blocks, wk, wv):
    return pl.pallas_call(
        pairs_kernel,
        out_shape=[shape((4 * ROWS, wk.shape[1]))] * 2,
        in_specs=[VM] * 6,
        out_specs=[VM] * 2,
        compiler_params=params(5),
        cost_estimate=cost(3.8e9, 9e6),
        name="pair_kv",
    )(*blocks, wk, wv)


def attend_stretch(place_ref, ids_ref, q, k_ref, v_ref, u, col):
    cols = pl.ds(col, 2 * HD)
    at = [pl.ds(pl.multiple_of((ids_ref[j, u] ^ (2 * place_ref[0])) * R, R), R) for j in range(2)]
    zero = jnp.zeros((C, HD), LOW)
    both = jnp.concatenate(
        [jnp.concatenate([q[:, :HD], zero], axis=1), jnp.concatenate([zero, q[:, HD:]], axis=1)], axis=0
    )
    keys = jnp.concatenate([k_ref[at[0], cols], k_ref[at[1], cols]], axis=0)
    values = jnp.concatenate([v_ref[at[0], cols], v_ref[at[1], cols]], axis=0)
    s = nt(both, keys) * HD ** (-0.5)
    ex = jnp.exp(s - jnp.max(s, axis=-1, keepdims=True))
    p = (ex * (1.0 / jnp.sum(ex, axis=-1, keepdims=True))).astype(LOW)
    out = nn(p, values)
    return jnp.concatenate([out[:C, :HD], out[C:, HD:]], axis=1)


def last_kernel(place_ref, ids_ref, q_ref, qin_ref, k_ref, v_ref, send_ref, mine_ref, qf):
    qf[:8, :] = q_ref[ROWS - 16 :, :].astype(WIDE)[8:, :]
    qf[8:, :] = qin_ref[...].astype(WIDE)

    @pl.loop(0, q_ref.shape[1] // (2 * HD), unroll=2)
    def _(i):
        col = pl.multiple_of(i * 2 * HD, 2 * HD)
        cols = pl.ds(col, 2 * HD)
        q = qf[7 : 7 + C, cols].astype(LOW)
        out = attend_stretch(place_ref, ids_ref, q, k_ref, v_ref, 3, col)
        mine_ref[:, cols] = jnp.broadcast_to(out[:1], (8, 2 * HD))
        send_ref[:, cols] = jnp.concatenate([out[1:], jnp.zeros((1, 2 * HD), WIDE)], axis=0).astype(LOW)


def attend_last(at, ids, q, q_in, k, v):
    width = q.shape[1]
    return pl.pallas_call(
        last_kernel,
        out_shape=[shape((C, width)), shape((8, width), WIDE)],
        in_specs=[SM, SM] + [VM] * 4,
        out_specs=[VM] * 2,
        scratch_shapes=[pltpu.VMEM((8 + C, width), WIDE)],
        compiler_params=params(3),
        cost_estimate=cost(1.4e8, 5e6),
        name="attend_last",
    )(at, ids, q, q_in, k, v)


def rest_kernel(place_ref, ids_ref, q_ref, mine_ref, k_ref, v_ref, ctx_ref, qf, of):
    qf[...] = q_ref[...].astype(WIDE)
    of[: C, :] = jnp.zeros((C, of.shape[1]), WIDE)

    @pl.loop(0, q_ref.shape[1] // (2 * HD))
    def _(i):
        col = pl.multiple_of(i * 2 * HD, 2 * HD)
        cols = pl.ds(col, 2 * HD)
        for u in range(3):
            lo = C - 1 + C * u
            of[lo : lo + C, cols] = attend_stretch(place_ref, ids_ref, qf[lo : lo + C, cols].astype(LOW), k_ref, v_ref, u, col)
        of[ROWS - 1 :, cols] = mine_ref[:1, cols]

    token = lax.broadcasted_iota(jnp.int32, of.shape, 0)
    position = (place_ref[1] * ROWS + token + C) & (SEQ_LEN - 1)
    ctx_ref[...] = jnp.where(position >= C - 1, of[...], 0.0).astype(LOW)


def attend_rest(at, ids, q, mine, k, v):
    width = q.shape[1]
    return pl.pallas_call(
        rest_kernel,
        out_shape=shape((ROWS, width)),
        in_specs=[SM, SM] + [VM] * 4,
        out_specs=VM,
        scratch_shapes=[pltpu.VMEM((ROWS, width), WIDE)] * 2,
        compiler_params=params(5),
        cost_estimate=cost(4e8, 6e6),
        name="attend_rest",
    )(at, ids, q, mine, k, v)


def project_kernel(r, e_ref, ctx_ref, ret_ref, w_ref, out_ref):
    width = out_ref.shape[1]
    full = jnp.concatenate([ctx_ref[:C, :] + ret_ref[...], ctx_ref[C:, :]], axis=0)
    for c0 in range(0, width, 512):
        cols = pl.ds(pl.multiple_of((e_ref[0] ^ r) * width + c0, 512), 512)
        out_ref[:, c0 : c0 + 512] = nn(full, w_ref[:, cols]).astype(out_ref.dtype)


def project(e, ctx, returned, w, r, kind):
    return pl.pallas_call(
        functools.partial(project_kernel, r),
        out_shape=shape(ctx.shape, kind),
        in_specs=[SM] + [VM] * 3,
        out_specs=VM,
        compiler_params=params(4),
        cost_estimate=cost(5.4e8, 3e6),
    )(e, ctx, returned, w)


def total_kernel(e_ref, hidden_ref, a_ref, b_ref, c_ref, out_ref):
    width = out_ref.shape[1]
    cols = pl.ds(pl.multiple_of(e_ref[0] * width, 128), width)
    branch = a_ref[...] + b_ref[...].astype(WIDE) + c_ref[...].astype(WIDE)
    out_ref[...] = (hidden_ref[:, cols].astype(WIDE) + branch).astype(LOW)


def total(e, hidden, a, b, c):
    return pl.pallas_call(
        total_kernel,
        out_shape=shape(a.shape),
        in_specs=[SM] + [VM] * 4,
        out_specs=VM,
        compiler_params=params(4),
        cost_estimate=cost(1e6, 3e6),
        name="total",
    )(e, hidden, a, b, c)


def sum_kernel(own_ref, a_ref, b_ref, c_ref, *refs):
    whole = refs[-1]
    whole[...] = own_ref[...] + a_ref[...].astype(WIDE) + b_ref[...].astype(WIDE) + c_ref[...].astype(WIDE)
    size = own_ref.shape[0] // 4
    for k, out in enumerate(refs[:-1]):
        out[...] = whole[k * size : (k + 1) * size, :].astype(out.dtype)


def summed(own, got):
    rows, width = own.shape
    return pl.pallas_call(
        sum_kernel,
        out_shape=[shape((rows // 4, width), WIDE)] + [shape((rows // 4, width))] * 3,
        in_specs=[VM] * 4,
        out_specs=[VM] * 4,
        scratch_shapes=[pltpu.VMEM((rows, width), WIDE)],
        compiler_params=params(4),
        cost_estimate=cost(2e6, 4e6),
    )(own, *got)


def last_sum_kernel(own_ref, a_ref, b_ref, c_ref, *outs):
    whole = own_ref[...] + a_ref[...].astype(WIDE) + b_ref[...].astype(WIDE) + c_ref[...].astype(WIDE)
    for m, out in enumerate(outs):
        out[...] = whole[:, m * DE : (m + 1) * DE] * (1.0 / 256)


def last_sum(own, got):
    return pl.pallas_call(
        last_sum_kernel,
        out_shape=[shape((own.shape[0], DE), WIDE)] * 4,
        in_specs=[VM] * 4,
        out_specs=[VM] * 4,
        compiler_params=params(2),
        cost_estimate=cost(1e5, 4e5),
        name="last_sum",
    )(own, *got)


def exchanged(chunks, pairs):
    return [sent(chunks[k - 1], pairs[k]) for k in (2, 1, 3)]


def on_device(
    hidden,
    dec_gain,
    cca_query,
    cca_key,
    cca_value,
    cca_out,
    neighbours,
    enc_gain,
    enc_query,
    enc_key,
    enc_value,
    enc_output,
    enc_cotangent,
    neighbour_ids,
):
    enc_index, seq_index = lax.axis_index("enc"), lax.axis_index("seq")
    e = enc_index.astype(jnp.int32).reshape(1)
    own = (enc_query, enc_key, enc_value, enc_output)
    far = [sent(m, ACROSS_Y) for m in own]
    near = [sent(m, SIBLING) for m in own]
    far_near = [sent(m, SIBLING) for m in far]

    def shards(lo):
        return [m for group in (own, near, far, far_near) for m in group[lo : lo + 2]]

    queries = query_projection(hidden, dec_gain, cca_query)
    q_in = shifted(queries[:C], "seq", -1)

    x = neighbours.reshape(ROWS, DE)
    cot = enc_cotangent.reshape(ROWS, DE)
    norm, picks, norm_t = prepare(x, enc_gain, gradient_row_order())
    q, k, p, w_qk = encode_scores(e, queries, norm, shards(0))
    encoded, v, ctx, w_vo = encode_values(e, x, norm, p, shards(2))
    far_nb = sent(encoded, PARTNER)
    near_nb = sent(encoded, SIBLING)
    d, g_other, ctx_t = backward(cot, q, k, v, ctx, p, w_vo, picks, norm_t)
    received = sent(g_other, SIBLING)
    d_input = finish(x, enc_gain, cot, d, w_qk, w_vo)
    own_rows, *chunks = own_gradients(norm_t, ctx_t, d, cot, received)
    far_near_nb = sent(far_nb, SIBLING)

    ids = neighbour_ids.T
    at = jnp.stack([enc_index, seq_index]).astype(jnp.int32)
    keys, values = pair_kv((encoded, near_nb, far_nb, far_near_nb), cca_key, cca_value)
    to_next, mine = attend_last(at, ids, queries, q_in, keys, values)
    returned = shifted(to_next, "seq", 1)
    context = attend_rest(at, ids, queries, mine, keys, values)

    got3 = sent(project(e, context, returned, cca_out, 3, LOW), SIBLING)
    part2 = project(e, context, returned, cca_out, 2, WIDE)
    got2 = sent((part2 + got3.astype(WIDE)).astype(LOW), PARTNER)
    got1 = sent(project(e, context, returned, cca_out, 1, LOW), SIBLING)
    part0 = project(e, context, returned, cca_out, 0, WIDE)

    got = exchanged(chunks, FIRST)
    own_rows, *chunks = summed(own_rows, got)
    got = exchanged(chunks, SECOND)
    own_rows, *chunks = summed(own_rows, got)
    got = exchanged(chunks, THIRD)
    grads = last_sum(own_rows, got)
    mixed = total(e, hidden, part0, got1, got2)
    return (mixed, d_input.reshape(neighbours.shape), grads[0], grads[1], grads[2], grads[3])


def solution(mesh):
    return jax.shard_map(
        on_device,
        mesh=mesh,
        in_specs=(
            P("seq", None),
            P(),
            P(None, "enc"),
            P(None, "enc"),
            P(None, "enc"),
            P("enc", None),
            P("seq", "enc", None, None),
            P(),
            P("enc", None),
            P("enc", None),
            P("enc", None),
            P("enc", None),
            P("seq", "enc", None, None),
            P("seq", None),
        ),
        out_specs=(
            P("seq", "enc"),
            P("seq", "enc", None, None),
            P(("enc", "seq"), None),
            P(("enc", "seq"), None),
            P(("enc", "seq"), None),
            P(("enc", "seq"), None),
        ),
        check_vma=False,
    )
```
